32 devices in a mesh: expert: 8 (over z, core), dp: 4 (over y, x).
Axes of the slice: x: 2, y: 2, z: 4, core: 2. Of those that a mesh axis runs over, the one named last changes fastest.
Arguments:
- tokens: bfloat16 [4096, 1024], P(('expert', 'dp')), may hold values from -6 to 6
- out_grad: bfloat16 [4096, 1024], P(('expert', 'dp')), may hold values from -0.59765625 to 0.59765625
- expert_ids: int32 [4096, 3], P(('expert', 'dp')), may hold values from 0 to 7, all different within a row; in each aligned block of 128 rows (0 to 127, 128 to 255, ...) at most 64 rows name the same one
- gate_probs: float32 [4096, 3], P(('expert', 'dp')), may hold values from 0.05 to 0.5
- w_gate: bfloat16 [8, 1024, 384], P('expert'), may hold values from -0.1875 to 0.1875
- w_up: bfloat16 [8, 1024, 384], P('expert'), may hold values from -0.1875 to 0.1875
- w_down: bfloat16 [8, 384, 1024], P('expert'), may hold values from -0.3125 to 0.3125
Outputs:
- grad_gate: bfloat16 [8, 1024, 384], P('expert', 'dp')
- grad_up: bfloat16 [8, 1024, 384], P('expert', 'dp')
- grad_down: bfloat16 [8, 384, 1024], P('expert', 'dp')
The draws below stay inside these ranges and needn't reach their ends.
Inputs may be any that keep to these rules, and one draw needn't show every extreme that they name: `expert_ids`: each row names 3 different experts. In the 128 rows of one device no expert is named by more than 64 rows, a bound that some block reaches.
All inputs are finite; a program needn't handle non-finite values.
Results may differ from the reference program's by a relative error of at most 0.018.
Values may be sent and summed in bfloat16 or wider, within the bound.
A program may use at most 64 MiB of HBM per device.

```python
import math
import jax
import jax.numpy as jnp
import numpy as np
from jax import lax

D = 1024
H = 384
TOP = 3
TOK_DEV = 128
EXPERTS = 8
CAP = 64
TOKENS = 4096
N_EXPERT = 8
N_DP = 4


def shard_levels(own_key, dims, split, least, largest):
    def one(position, parts):
        draws = jax.random.uniform(jax.random.fold_in(jax.random.fold_in(own_key, 6), position), (parts,), jnp.float32, least / len(split), largest / len(split))
        return jnp.repeat(jnp.exp(draws), dims[position] // parts).reshape((-1,) + (1,) * (len(dims) - position - 1))

    loudness = one(*split[0])
    for cut in split[1:]:
        loudness = loudness * one(*cut)
    return loudness


def deal_out(key, own, number, rows, amount, top, most, slope):
    sequence = jax.random.permutation(key, amount)
    packed, common = portions_of(amount, rows * top, most, slope, True), portions_of(amount, rows * top, most, slope, False)
    places = jnp.arange(amount)

    def named(lengths, offset_by):
        used = int((lengths > 0).sum())
        fixed = max(1, used // 4)
        shifted = fixed + (places - fixed + offset_by * (used - fixed)) % max(1, amount - fixed)
        return jnp.zeros((amount,), jnp.int32).at[sequence[jnp.where(places < fixed, places, shifted)]].set(jnp.asarray(lengths, jnp.int32))

    lengths = jnp.where(number % 4 == 0, named(packed, number // 4), named(common, number - number // 4 - 1))
    mixed = jax.random.permutation(jax.random.fold_in(own, 3), amount)
    donor, taker = mixed[0:amount // 2 * 2:2], mixed[1:amount // 2 * 2:2]
    margin = jnp.minimum(lengths[donor] - 1, most - lengths[taker]) // 2
    margin = jnp.where((donor == sequence[0]) | (taker == sequence[0]) | (lengths[taker] == 0), 0, jnp.maximum(margin, 0))
    shifted = jax.random.randint(jax.random.fold_in(own, 4), (amount // 2,), 0, 1 << 20) % (margin + 1)
    lengths = lengths.at[donor].add(-shifted).at[taker].add(shifted)
    items = jnp.searchsorted(jnp.cumsum(lengths), jnp.arange(rows * top), side="right").astype(jnp.int32)
    listing = items.reshape(top, rows).T
    listing = listing[jax.random.permutation(jax.random.fold_in(own, 1), rows)]
    offset_by = jax.random.randint(jax.random.fold_in(own, 2), (rows, 1), 0, top)
    return jnp.take_along_axis(listing, (jnp.arange(top)[None, :] + offset_by) % top, axis=1)


def portions_of(count, total, most, lean, full):
    loads = [(1 << 20) // math.isqrt(rank ** lean) + 1 for rank in range(1, count + 1)]
    largest = most if full else min(most, max(-(-total // count), total * loads[0] // sum(loads)))
    least = 1 if total - largest >= count - 1 else 0
    given, rest = [largest] + [least] * (count - 1), total - largest - least * (count - 1)
    while rest > 0:
        movable = [i for i in range(1, count) if given[i] < largest] or [i for i in range(1, count) if given[i] < most]
        mass, left = sum([loads[i] for i in movable]), rest
        for i in movable:
            more = min(most - given[i], max(1, left * loads[i] // mass), rest)
            given[i] = given[i] + more
            rest = rest - more
    return np.array(given)


def scatter_about(rng, extent, width, most, cuts=(), dtype=jnp.bfloat16):
    result = jax.random.normal(rng, extent, jnp.float32) * width
    if len(cuts) > 0:
        result = shard_levels(rng, extent, cuts, -0.22, 0.18) * result
    return jnp.clip(result, min=-most, max=most).astype(dtype)


def setup_inputs(seed: int = 0) -> dict:
    splits = jax.random.split(jax.random.key(seed), 8)
    tokens = scatter_about(splits[0], (TOKENS, D), 1.0, 6.0, ((0, 32),))
    out_grad = scatter_about(splits[1], (TOKENS, D), 0.1, 0.59765625, ((0, 32),))
    expert_ids_keys = jax.random.split(jax.random.fold_in(splits[2], 1), TOKENS // TOK_DEV)
    expert_ids_turns = jax.random.permutation(jax.random.fold_in(splits[2], 3), TOKENS // TOK_DEV)
    expert_ids = jax.vmap(lambda own, number: deal_out(jax.random.fold_in(splits[2], 2), own, number, TOK_DEV, EXPERTS, TOP, CAP, 2))(expert_ids_keys, expert_ids_turns).reshape((TOKENS, TOP))
    gate_probs = jnp.clip(0.05 + 0.45 * jax.random.uniform(splits[3], (TOKENS, TOP), jnp.float32) ** shard_levels(splits[3], (TOKENS, TOP), ((0, 32),), -0.2, 0.2), 0.05, 0.5)
    w_gate = scatter_about(splits[4], (EXPERTS, D, H), D ** -0.5, 0.1875, ((0, 8),))
    w_up = scatter_about(splits[5], (EXPERTS, D, H), D ** -0.5, 0.1875, ((0, 8),))
    w_down = scatter_about(splits[6], (EXPERTS, H, D), H ** -0.5, 0.3125, ((0, 8),))
    return dict(tokens=tokens, out_grad=out_grad, expert_ids=expert_ids, gate_probs=gate_probs, w_gate=w_gate, w_up=w_up, w_down=w_down)


def expert_grads(rows_in, rows_grad, gate_w, up_w, down_w):
    gate_pre = jnp.dot(rows_in, gate_w, preferred_element_type=jnp.float32)
    up_pre = jnp.dot(rows_in, up_w, preferred_element_type=jnp.float32)
    sigma = jax.nn.sigmoid(gate_pre)
    active = gate_pre * sigma
    hidden = (active * up_pre).astype(jnp.bfloat16)
    grad_down = lax.dot_general(hidden, rows_grad, (((0,), (0,)), ((), ())), preferred_element_type=jnp.float32)
    grad_hidden = lax.dot_general(rows_grad, down_w, (((1,), (1,)), ((), ())), preferred_element_type=jnp.float32)
    grad_upper = (grad_hidden * active).astype(jnp.bfloat16)
    grad_gate_pre = (grad_hidden * up_pre * sigma * (1.0 + gate_pre * (1.0 - sigma))).astype(jnp.bfloat16)
    grad_gate = lax.dot_general(rows_in, grad_gate_pre, (((0,), (0,)), ((), ())), preferred_element_type=jnp.float32)
    grad_up = lax.dot_general(rows_in, grad_upper, (((0,), (0,)), ((), ())), preferred_element_type=jnp.float32)
    return grad_gate, grad_up, grad_down


def regroup(array):
    tail = array.shape[1:]
    shaped = array.reshape((N_EXPERT, N_DP, TOK_DEV) + tail)
    shaped = jnp.swapaxes(shaped, 0, 1)
    return shaped.reshape((N_DP, N_EXPERT * TOK_DEV) + tail)


def reference(tokens, out_grad, expert_ids, gate_probs, w_gate, w_up, w_down):
    group_tokens = regroup(tokens)
    group_cot = regroup(out_grad)
    group_ids = regroup(expert_ids)
    group_probs = regroup(gate_probs)
    limit = N_EXPERT * CAP

    def one_group(carry, inputs):
        tok_block, cot_block, id_block, prob_block = inputs
        flat_ids = id_block.reshape(-1)
        flat_probs = prob_block.reshape(-1)

        def one_expert(expert):
            chosen = flat_ids == expert
            picked = jnp.nonzero(chosen, size=limit, fill_value=0)[0]
            valid = jnp.arange(limit) < jnp.sum(chosen.astype(jnp.int32))
            token_row = picked // TOP
            rows_in = jnp.where(valid[:, None], tok_block[token_row], jnp.zeros((), jnp.bfloat16)).astype(jnp.bfloat16)
            scaled = flat_probs[picked][:, None] * cot_block[token_row].astype(jnp.float32)
            scaled = jnp.where(valid[:, None], scaled, jnp.zeros((), jnp.float32)).astype(jnp.bfloat16)
            grads = expert_grads(rows_in, scaled, w_gate[expert], w_up[expert], w_down[expert])
            return (grads[0].astype(jnp.bfloat16), grads[1].astype(jnp.bfloat16), grads[2].astype(jnp.bfloat16))

        stacked = lax.map(one_expert, jnp.arange(EXPERTS))
        carry = (carry[0] + stacked[0].astype(jnp.float32), carry[1] + stacked[1].astype(jnp.float32), carry[2] + stacked[2].astype(jnp.float32))
        return carry, None

    start = (jnp.zeros((EXPERTS, D, H), jnp.float32), jnp.zeros((EXPERTS, D, H), jnp.float32), jnp.zeros((EXPERTS, H, D), jnp.float32))
    totals, _ = lax.scan(one_group, start, (group_tokens, group_cot, group_ids, group_probs))
    return totals[0].astype(jnp.bfloat16), totals[1].astype(jnp.bfloat16), totals[2].astype(jnp.bfloat16)
```

```python
import functools

import jax
import jax.numpy as jnp
from jax import lax
from jax.experimental import pallas as pl
from jax.experimental.pallas import tpu as pltpu
from jax.sharding import PartitionSpec as P

MESH = pl.DeviceIdType.MESH
CORES = 2


def kernel(
    n_e, n_d,
    tok, cot, ids, probs, wg_in, wu_in, wd_in,
    out_g, out_u, out_d,
    X, G, PT, WG, WU, WD, XT, HT, GG, S, SB, SD, RB, RD, ACC, ACD,
    lsem, chain_s, sib_s, blk_r, rs_s, rs_r,
):
    rows, width = tok.shape
    hid = wg_in.shape[2]
    top = ids.shape[0]
    n_z = n_e // CORES
    me = lax.axis_index("expert")
    dd = lax.axis_index("dp")
    z, c = me // CORES, me % CORES
    sib = z * CORES + (1 - c)

    erow = lax.broadcasted_iota(jnp.int32, PT.shape[1:], 0)
    table = jnp.zeros(PT.shape[1:], jnp.float32)
    for k in range(top):
        table = table + jnp.where(ids[k : k + 1, :] == erow, probs[k : k + 1, :], 0.0)
    PT[me] = table

    barrier = pltpu.get_barrier_semaphore()
    for step in (-1, 1):
        @pl.when(jnp.logical_and(z + step >= 0, z + step < n_z))
        def _():
            pl.semaphore_signal(barrier, inc=1, device_id={"expert": me + step * CORES}, device_id_type=MESH)
    pl.semaphore_signal(barrier, inc=1, device_id={"expert": sib}, device_id_type=MESH)
    for i in range(1, n_d):
        pl.semaphore_signal(barrier, inc=1, device_id={"dp": (dd + i) % n_d}, device_id_type=MESH)
    arrivals = n_d + jnp.where(z > 0, 1, 0) + jnp.where(z < n_z - 1, 1, 0)
    pl.semaphore_wait(barrier, arrivals)

    full = (PT, X, G)
    own = (PT.at[me], tok, cot)

    def hop(k, d, src, mine):
        there = me + (CORES if d == 0 else -CORES)
        return pltpu.make_async_remote_copy(
            src_ref=own[k] if mine else full[k].at[src],
            dst_ref=full[k].at[src],
            send_sem=chain_s.at[k, d, src],
            recv_sem=blk_r.at[k, src],
            device_id={"expert": there},
            device_id_type=MESH,
        )

    def across(k, src, mine):
        return pltpu.make_async_remote_copy(
            src_ref=own[k] if mine else full[k].at[src],
            dst_ref=full[k].at[src],
            send_sem=sib_s.at[k, src],
            recv_sem=blk_r.at[k, src],
            device_id={"expert": sib},
            device_id_type=MESH,
        )

    def can(d):
        return z < n_z - 1 if d == 0 else z > 0

    for k in range(3):
        for d in range(2):
            @pl.when(can(d))
            def _():
                hop(k, d, me, True).start()
        across(k, me, True).start()
    local = [
        pltpu.make_async_copy(tok, X.at[me], lsem.at[0]),
        pltpu.make_async_copy(cot, G.at[me], lsem.at[1]),
        pltpu.make_async_copy(wg_in.at[0], WG, lsem.at[2]),
        pltpu.make_async_copy(wu_in.at[0], WU, lsem.at[3]),
        pltpu.make_async_copy(wd_in.at[0], WD, lsem.at[4]),
    ]
    for copy in local:
        copy.start()
    for copy in local:
        copy.wait()

    pair = CORES * rows

    def forward(zz):
        for k in range(3):
            across(k, zz * CORES + (1 - c), False).wait_recv()
        at = pl.multiple_of(zz * pair, pair)
        x = X[pl.ds(zz * CORES, CORES)].reshape(pair, width)
        XT[:, pl.ds(at, pair)] = x.T
        parts = []
        for h in range(CORES):
            p = PT[zz * CORES + h, pl.ds(me, 1), :]
            p = jnp.broadcast_to(p, (rows, rows)).T[:, :1]
            parts.append((p * G[zz * CORES + h].astype(jnp.float32)).astype(jnp.bfloat16))
        scaled = jnp.concatenate(parts, axis=0)
        S[pl.ds(at, pair), :] = scaled
        gate = jnp.dot(x, WG[...], preferred_element_type=jnp.float32)
        up = jnp.dot(x, WU[...], preferred_element_type=jnp.float32)
        gh = lax.dot_general(scaled, WD[...], (((1,), (1,)), ((), ())), preferred_element_type=jnp.float32)
        sigma = jax.nn.sigmoid(gate)
        active = gate * sigma
        HT[:, pl.ds(at, pair)] = (active * up).astype(jnp.bfloat16).T
        GG[pl.ds(at, pair), hid:] = (gh * active).astype(jnp.bfloat16)
        GG[pl.ds(at, pair), :hid] = (gh * up * sigma * (1.0 + gate * (1.0 - sigma))).astype(jnp.bfloat16)

    @pl.loop(0, n_z)
    def _(s):
        @pl.loop(0, 2)
        def _(d):
            zz = jnp.where(d == 0, z - s, z + s)

            @pl.when((zz >= 0) & (zz < n_z) & ((s > 0) | (d == 0)))
            def _():
                forward(zz)

        for k in range(3):
            for d in range(2):
                zz = z - (s + 1) if d == 0 else z + (s + 1)
                src = zz * CORES + c

                @pl.when((zz >= 0) & (zz < n_z))
                def _():
                    hop(k, d, src, False).wait_recv()

                    @pl.when(can(d))
                    def _():
                        hop(k, d, src, False).start()

                    across(k, src, False).start()

    piece, hpiece = width // n_d, hid // n_d
    chunk = max(piece, min(256, width))
    n_c = width // chunk
    hchunk, per = hid // n_c, chunk // piece

    def give(k, j, slot):
        src = SB.at[pl.ds(pl.multiple_of(j * piece, piece), piece)] if k == 0 else SD.at[j]
        dst = RB.at[slot] if k == 0 else RD.at[slot]
        return pltpu.make_async_remote_copy(
            src_ref=src, dst_ref=dst, send_sem=rs_s.at[k, j], recv_sem=rs_r.at[k, slot],
            device_id={"dp": j}, device_id_type=MESH,
        )

    @pl.loop(0, n_c)
    def _(i):
        cc = (dd // per + 1 + i) % n_c
        at = pl.multiple_of(cc * chunk, chunk)
        hat = pl.multiple_of(cc * hchunk, hchunk)
        SB[pl.ds(at, chunk), :] = jnp.dot(
            XT[pl.ds(at, chunk), :], GG[...], preferred_element_type=jnp.float32
        ).astype(jnp.bfloat16)
        down = jnp.dot(HT[pl.ds(hat, hchunk), :], S[...], preferred_element_type=jnp.float32).astype(jnp.bfloat16)
        for q in range(per):
            SD[cc * per + q] = down[q * hpiece : (q + 1) * hpiece]
        for q in range(per):
            j = cc * per + q

            @pl.when(j != dd)
            def _():
                give(0, j, dd).start()
                give(1, j, dd).start()

    ACC[...] = SB[pl.ds(pl.multiple_of(dd * piece, piece), piece), :].astype(jnp.float32)
    ACD[...] = SD[dd].astype(jnp.float32)

    @pl.loop(1, n_d)
    def _(i):
        j = (dd + n_d - i) % n_d
        give(0, (dd + 1) % n_d, j).wait_recv()
        ACC[...] += RB[j].astype(jnp.float32)
        give(1, (dd + 1) % n_d, j).wait_recv()
        ACD[...] += RD[j].astype(jnp.float32)

    out_g[0] = ACC[:, :hid].astype(jnp.bfloat16)
    out_u[0] = ACC[:, hid:].astype(jnp.bfloat16)
    out_d[0] = ACD[...].astype(jnp.bfloat16)

    @pl.loop(1, n_d)
    def _(i):
        j = (dd + i) % n_d
        give(0, j, dd).wait_send()
        give(1, j, dd).wait_send()

    @pl.loop(0, n_z)
    def _(s):
        for k in range(3):
            for d in range(2):
                zz = z - s if d == 0 else z + s
                src = zz * CORES + c

                @pl.when((zz >= 0) & (zz < n_z) & can(d))
                def _():
                    hop(k, d, src, False).wait_send()

            across(k, s * CORES + c, False).wait_send()


def solution(mesh):
    n_e, n_d = mesh.shape["expert"], mesh.shape["dp"]

    def step(tokens, out_grad, expert_ids, gate_probs, w_gate, w_up, w_down):
        rows, width = tokens.shape
        hid = w_gate.shape[2]
        total = n_e * rows
        lanes = -(-n_e // 8) * 8
        bf, f32 = jnp.bfloat16, jnp.float32
        vmem = pl.BlockSpec(memory_space=pltpu.VMEM)
        hbm = pl.BlockSpec(memory_space=pl.ANY)
        piece, hpiece = width // n_d, hid // n_d
        dma = pltpu.SemaphoreType.DMA
        return pl.pallas_call(
            functools.partial(kernel, n_e, n_d),
            out_shape=(
                jax.ShapeDtypeStruct((1, piece, hid), bf),
                jax.ShapeDtypeStruct((1, piece, hid), bf),
                jax.ShapeDtypeStruct((1, hpiece, width), bf),
            ),
            in_specs=[hbm, hbm, vmem, vmem, hbm, hbm, hbm],
            out_specs=(vmem, vmem, vmem),
            scratch_shapes=[
                pltpu.VMEM((n_e, rows, width), bf),
                pltpu.VMEM((n_e, rows, width), bf),
                pltpu.VMEM((n_e, lanes, rows), f32),
                pltpu.VMEM((width, hid), bf),
                pltpu.VMEM((width, hid), bf),
                pltpu.VMEM((hid, width), bf),
                pltpu.VMEM((width, total), bf),
                pltpu.VMEM((hid, total), bf),
                pltpu.VMEM((total, 2 * hid), bf),
                pltpu.VMEM((total, width), bf),
                pltpu.VMEM((width, 2 * hid), bf),
                pltpu.VMEM((n_d, hpiece, width), bf),
                pltpu.VMEM((n_d, piece, 2 * hid), bf),
                pltpu.VMEM((n_d, hpiece, width), bf),
                pltpu.VMEM((piece, 2 * hid), f32),
                pltpu.VMEM((hpiece, width), f32),
                dma((5,)),
                dma((3, 2, n_e)),
                dma((3, n_e)),
                dma((3, n_e)),
                dma((2, n_d)),
                dma((2, n_d)),
            ],
            compiler_params=pltpu.CompilerParams(
                collective_id=0, has_side_effects=True, vmem_limit_bytes=60 * 1024 * 1024
            ),
        )(tokens, out_grad, expert_ids.T, gate_probs.T, w_gate, w_up, w_down)

    spread = P(("expert", "dp"), None)
    return jax.shard_map(
        step,
        mesh=mesh,
        in_specs=(spread, spread, spread, spread) + (P("expert", None, None),) * 3,
        out_specs=(P("expert", "dp", None),) * 3,
        check_vma=False,
    )
```

```python
import functools
import math

import jax
import jax.numpy as jnp
from jax import lax
from jax.experimental import pallas as pl
from jax.experimental.pallas import tpu as pltpu
from jax.sharding import PartitionSpec as P

MESH = pl.DeviceIdType.MESH
CORES = 2


def kernel(
    n_e, n_a, n_b,
    tok, cot, ids, probs, wg_in, wu_in, wd_in,
    out_g, out_u, out_d,
    X, G, PT, WG, WU, WD, GU, XT, HT, GG, S, MB, DB, MR, DR, MP, DP, MQ, DQ,
    lsem, chain_s, sib_s, blk_r, one_s, one_r, two_s, two_r,
):
    n_d = n_a * n_b
    rows, width = tok.shape
    hid = wg_in.shape[2]
    top = ids.shape[0]
    n_z = n_e // CORES
    me = lax.axis_index("expert")
    dd = lax.axis_index("dp")
    z, c = me // CORES, me % CORES
    sib = z * CORES + (1 - c)

    erow = lax.broadcasted_iota(jnp.int32, PT.shape[1:], 0)
    table = jnp.zeros(PT.shape[1:], jnp.float32)
    for k in range(top):
        table = table + jnp.where(ids[k : k + 1, :] == erow, probs[k : k + 1, :], 0.0)
    PT[me] = table

    barrier = pltpu.get_barrier_semaphore()
    for step in (-1, 1):
        @pl.when(jnp.logical_and(z + step >= 0, z + step < n_z))
        def _():
            pl.semaphore_signal(barrier, inc=1, device_id={"expert": me + step * CORES}, device_id_type=MESH)
    pl.semaphore_signal(barrier, inc=1, device_id={"expert": sib}, device_id_type=MESH)
    for i in range(1, n_a):
        pl.semaphore_signal(barrier, inc=1, device_id={"dp": ((dd // n_b + i) % n_a) * n_b + dd % n_b}, device_id_type=MESH)
    for i in range(1, n_b):
        pl.semaphore_signal(barrier, inc=1, device_id={"dp": dd // n_b * n_b + (dd % n_b + i) % n_b}, device_id_type=MESH)
    arrivals = n_a + n_b - 1 + jnp.where(z > 0, 1, 0) + jnp.where(z < n_z - 1, 1, 0)
    pl.semaphore_wait(barrier, arrivals)

    full = (PT, X, G)
    own = (PT.at[me], tok, cot)

    def hop(k, d, src, mine):
        there = me + (CORES if d == 0 else -CORES)
        return pltpu.make_async_remote_copy(
            src_ref=own[k] if mine else full[k].at[src],
            dst_ref=full[k].at[src],
            send_sem=chain_s.at[k, d, src],
            recv_sem=blk_r.at[k, src],
            device_id={"expert": there},
            device_id_type=MESH,
        )

    def across(k, src, mine):
        return pltpu.make_async_remote_copy(
            src_ref=own[k] if mine else full[k].at[src],
            dst_ref=full[k].at[src],
            send_sem=sib_s.at[k, src],
            recv_sem=blk_r.at[k, src],
            device_id={"expert": sib},
            device_id_type=MESH,
        )

    def can(d):
        return z < n_z - 1 if d == 0 else z > 0

    for k in range(3):
        for d in range(2):
            @pl.when(can(d))
            def _():
                hop(k, d, me, True).start()
        across(k, me, True).start()
    local = [
        pltpu.make_async_copy(tok, X.at[me], lsem.at[0]),
        pltpu.make_async_copy(cot, G.at[me], lsem.at[1]),
        pltpu.make_async_copy(wg_in.at[0], WG, lsem.at[2]),
        pltpu.make_async_copy(wu_in.at[0], WU, lsem.at[3]),
        pltpu.make_async_copy(wd_in.at[0], WD, lsem.at[4]),
    ]
    for copy in local:
        copy.start()
    for copy in local:
        copy.wait()

    pair = CORES * rows

    def base(zz):
        return pl.multiple_of(zz * pair, pair)

    def forward_tokens(zz, d):
        for k in range(2):
            across(k, zz * CORES + (1 - c), False).wait_recv()
        x = X[pl.ds(zz * CORES, CORES)].reshape(pair, width)
        GU[d, :, :hid] = jnp.dot(x, WG[...], preferred_element_type=jnp.float32)
        GU[d, :, hid:] = jnp.dot(x, WU[...], preferred_element_type=jnp.float32)
        XT[:, pl.ds(base(zz), pair)] = x.T

    def forward_cots(zz, d):
        across(2, zz * CORES + (1 - c), False).wait_recv()
        at = base(zz)
        parts = []
        for h in range(CORES):
            p = PT[zz * CORES + h, pl.ds(me, 1), :]
            p = jnp.broadcast_to(p, (rows, rows)).T[:, :1]
            parts.append((p * G[zz * CORES + h].astype(jnp.float32)).astype(jnp.bfloat16))
        scaled = jnp.concatenate(parts, axis=0)
        S[pl.ds(at, pair), :] = scaled
        gh = lax.dot_general(scaled, WD[...], (((1,), (1,)), ((), ())), preferred_element_type=jnp.float32)
        gate, up = GU[d, :, :hid], GU[d, :, hid:]
        sigma = jax.nn.sigmoid(gate)
        active = gate * sigma
        GG[pl.ds(at, pair), :hid] = (gh * up * sigma * (1.0 + gate * (1.0 - sigma))).astype(jnp.bfloat16)
        GG[pl.ds(at, pair), hid:] = (gh * active).astype(jnp.bfloat16)
        HT[:, pl.ds(at, pair)] = (active * up).astype(jnp.bfloat16).T

    def both(s, work):
        @pl.loop(0, 2)
        def _(d):
            zz = jnp.where(d == 0, z - s, z + s)

            @pl.when((zz >= 0) & (zz < n_z) & ((s > 0) | (d == 0)))
            def _():
                work(zz, d)

    def pass_on(s, kinds):
        for k in kinds:
            for d in range(2):
                zz = z - s if d == 0 else z + s
                src = zz * CORES + c

                @pl.when((zz >= 0) & (zz < n_z))
                def _():
                    hop(k, d, src, False).wait_recv()

                    @pl.when(can(d))
                    def _():
                        hop(k, d, src, False).start()

                    across(k, src, False).start()

    @pl.loop(0, n_z)
    def _(s):
        @pl.when(s > 0)
        def _():
            pass_on(s, (0, 1))

        both(s, forward_tokens)

        @pl.when(s > 0)
        def _():
            pass_on(s, (2,))

        both(s, forward_cots)

    piece, hpiece = width // n_d, hid // n_d
    chunk = max(piece, min(256, width))
    n_c = width // chunk
    hchunk, per = hid // n_c, chunk // piece
    half = width // 2

    def index(p, second, first):
        return second * n_b + first if p == 0 else first * n_b + second

    def first_of(p, j):
        return j % n_b if p == 0 else j // n_b

    def second_of(p, j):
        return j // n_b if p == 0 else j % n_b

    def mpiece(p, j):
        return MB.at[p, pl.ds(pl.multiple_of(j * piece, piece), piece)]

    def one(p, t, j):
        mine, there = first_of(p, dd), second_of(p, j)
        return pltpu.make_async_remote_copy(
            src_ref=mpiece(p, j) if t == 0 else DB.at[p, j],
            dst_ref=(MR if t == 0 else DR).at[p, mine, there],
            send_sem=one_s.at[p, t, j],
            recv_sem=one_r.at[p, t, mine, there],
            device_id={"dp": index(p, second_of(p, dd), first_of(p, j))},
            device_id_type=MESH,
        )

    def one_from(p, t, first, second):
        dst = (MR if t == 0 else DR).at[p, first, second]
        return pltpu.make_async_remote_copy(
            src_ref=dst, dst_ref=dst,
            send_sem=one_s.at[p, t, 0],
            recv_sem=one_r.at[p, t, first, second],
            device_id={"dp": index(p, second_of(p, dd), first)},
            device_id_type=MESH,
        )

    def two(p, t, second, slot):
        return pltpu.make_async_remote_copy(
            src_ref=(MP if t == 0 else DP).at[p, second],
            dst_ref=(MQ if t == 0 else DQ).at[p, slot],
            send_sem=two_s.at[p, t, second],
            recv_sem=two_r.at[p, t, slot],
            device_id={"dp": index(p, second, first_of(p, dd))},
            device_id_type=MESH,
        )

    @pl.loop(0, n_c)
    def _(i):
        if per == 1:
            step_a, step_b = n_a - 1 - i // n_b, n_b - 1 - i % n_b
            cc = ((dd // n_b + step_a) % n_a) * n_b + (dd % n_b + step_b) % n_b
        else:
            cc = (dd // per + 1 + i) % n_c
        at = pl.multiple_of(cc * chunk, chunk)
        hat = pl.multiple_of(cc * hchunk, hchunk)
        up_gate = jnp.dot(
            XT[pl.ds(at, chunk), :], GG[...], preferred_element_type=jnp.float32
        ).astype(jnp.bfloat16)
        for p in range(2):
            MB[p, pl.ds(at, chunk), :] = up_gate[:, p * hid : (p + 1) * hid]
        for t in range(2):
            if t == 1:
                down = jnp.dot(
                    HT[pl.ds(hat, hchunk), :], S[...], preferred_element_type=jnp.float32
                ).astype(jnp.bfloat16)
                for p in range(2):
                    for q in range(per):
                        DB[p, cc * per + q] = down[q * hpiece : (q + 1) * hpiece, p * half : (p + 1) * half]
            for p in range(2):
                for q in range(per):
                    j = cc * per + q

                    @pl.when(first_of(p, j) != first_of(p, dd))
                    def _():
                        one(p, t, j).start()

    def partial(p, t, second):
        first = first_of(p, dd)
        count = n_b if p == 0 else n_a
        j = index(p, second, first)
        total = (mpiece(p, j)[...] if t == 0 else DB[p, j]).astype(jnp.float32)
        for i in range(1, count):
            other = (first + i) % count
            one_from(p, t, other, second).wait_recv()
            total = total + (MR if t == 0 else DR)[p, other, second].astype(jnp.float32)
        return total

    for t in range(2):
        for p in range(2):
            count = n_a if p == 0 else n_b

            @pl.loop(1, count)
            def _(i):
                second = (second_of(p, dd) + i) % count
                (MP if t == 0 else DP)[p, second] = partial(p, t, second).astype(jnp.bfloat16)
                two(p, t, second, second_of(p, dd)).start()

    for t in range(2):
        for p in range(2):
            count = n_a if p == 0 else n_b
            mine = second_of(p, dd)
            total = partial(p, t, mine)
            for i in range(1, count):
                other = (mine + i) % count
                two(p, t, other, other).wait_recv()
                total = total + (MQ if t == 0 else DQ)[p, other].astype(jnp.float32)
            if t == 0:
                (out_g, out_u)[p][0] = total.astype(jnp.bfloat16)
            else:
                out_d[0, :, p * half : (p + 1) * half] = total.astype(jnp.bfloat16)

    for p in range(2):
        for t in range(2):
            @pl.loop(0, n_d)
            def _(j):
                @pl.when(first_of(p, j) != first_of(p, dd))
                def _():
                    one(p, t, j).wait_send()

            count = n_a if p == 0 else n_b

            @pl.loop(1, count)
            def _(i):
                two(p, t, (second_of(p, dd) + i) % count, second_of(p, dd)).wait_send()

    @pl.loop(0, n_z)
    def _(s):
        for k in range(3):
            for d in range(2):
                zz = z - s if d == 0 else z + s
                src = zz * CORES + c

                @pl.when((zz >= 0) & (zz < n_z) & can(d))
                def _():
                    hop(k, d, src, False).wait_send()

            across(k, s * CORES + c, False).wait_send()


def solution(mesh):
    n_e, n_d = mesh.shape["expert"], mesh.shape["dp"]
    n_b = max(b for b in range(1, n_d + 1) if n_d % b == 0 and b * b <= n_d)
    n_a = n_d // n_b

    def step(tokens, out_grad, expert_ids, gate_probs, w_gate, w_up, w_down):
        rows, width = tokens.shape
        hid = w_gate.shape[2]
        total = n_e * rows
        lanes = -(-n_e // 8) * 8
        bf, f32 = jnp.bfloat16, jnp.float32
        vmem = pl.BlockSpec(memory_space=pltpu.VMEM)
        hbm = pl.BlockSpec(memory_space=pltpu.HBM)
        piece, hpiece = width // n_d, hid // n_d
        dma = pltpu.SemaphoreType.DMA
        scratch = [
            ((n_e, rows, width), bf),
            ((n_e, rows, width), bf),
            ((n_e, lanes, rows), f32),
            ((width, hid), bf),
            ((width, hid), bf),
            ((hid, width), bf),
            ((2, CORES * rows, 2 * hid), f32),
            ((width, total), bf),
            ((hid, total), bf),
            ((total, 2 * hid), bf),
            ((total, width), bf),
            ((2, width, hid), bf),
            ((2, n_d, hpiece, width // 2), bf),
            ((2, n_a, n_a, piece, hid), bf),
            ((2, n_a, n_a, hpiece, width // 2), bf),
            ((2, n_a, piece, hid), bf),
            ((2, n_a, hpiece, width // 2), bf),
            ((2, n_a, piece, hid), bf),
            ((2, n_a, hpiece, width // 2), bf),
        ]
        held = sum(math.prod(shape) * jnp.dtype(kind).itemsize for shape, kind in scratch)
        return pl.pallas_call(
            functools.partial(kernel, n_e, n_a, n_b),
            out_shape=(
                jax.ShapeDtypeStruct((1, piece, hid), bf),
                jax.ShapeDtypeStruct((1, piece, hid), bf),
                jax.ShapeDtypeStruct((1, hpiece, width), bf),
            ),
            in_specs=[hbm, hbm, vmem, vmem, hbm, hbm, hbm],
            out_specs=(vmem, vmem, vmem),
            scratch_shapes=[pltpu.VMEM(shape, kind) for shape, kind in scratch]
            + [
                dma((5,)),
                dma((3, 2, n_e)),
                dma((3, n_e)),
                dma((3, n_e)),
                dma((2, 2, n_d)),
                dma((2, 2, n_a, n_a)),
                dma((2, 2, n_a)),
                dma((2, 2, n_a)),
            ],
            compiler_params=pltpu.CompilerParams(
                collective_id=0, has_side_effects=True, vmem_limit_bytes=held + (10 << 20)
            ),
        )(tokens, out_grad, expert_ids.T, gate_probs.T, w_gate, w_up, w_down)

    spread = P(("expert", "dp"), None)
    return jax.shard_map(
        step,
        mesh=mesh,
        in_specs=(spread, spread, spread, spread) + (P("expert", None, None),) * 3,
        out_specs=(P("expert", "dp", None),) * 3,
        check_vma=False,
    )
```

```python
import functools
import math

import jax
import jax.numpy as jnp
from jax import lax
from jax.experimental import pallas as pl
from jax.experimental.pallas import tpu as pltpu
from jax.sharding import PartitionSpec as P

MESH = pl.DeviceIdType.MESH
CORES = 2


def kernel(
    n_e, n_a, n_b,
    tok, cot, ids_in, probs_in, wg_in, wu_in, wd_in,
    out_g, out_u, out_d,
    ids, probs, X, G, PT, WG, WU, WD, GU, XT, HT, GG, S, MB, DB, MR, DR, MP, DP, MQ, DQ,
    lsem, chain_s, sib_s, blk_r, one_s, one_r, two_s, two_r,
):
    n_d = n_a * n_b
    rows, width = tok.shape
    hid = wg_in.shape[2]
    top = ids_in.shape[0]
    n_z = n_e // CORES
    me = lax.axis_index("expert")
    dd = lax.axis_index("dp")
    z, c = me // CORES, me % CORES
    sib = z * CORES + (1 - c)

    barrier = pltpu.get_barrier_semaphore()
    for step in (-1, 1):
        @pl.when(jnp.logical_and(z + step >= 0, z + step < n_z))
        def _():
            pl.semaphore_signal(barrier, inc=1, device_id={"expert": me + step * CORES}, device_id_type=MESH)
    pl.semaphore_signal(barrier, inc=1, device_id={"expert": sib}, device_id_type=MESH)
    for i in range(1, n_a):
        pl.semaphore_signal(barrier, inc=1, device_id={"dp": ((dd // n_b + i) % n_a) * n_b + dd % n_b}, device_id_type=MESH)
    for i in range(1, n_b):
        pl.semaphore_signal(barrier, inc=1, device_id={"dp": dd // n_b * n_b + (dd % n_b + i) % n_b}, device_id_type=MESH)
    small = [
        pltpu.make_async_copy(ids_in, ids, lsem.at[5]),
        pltpu.make_async_copy(probs_in, probs, lsem.at[6]),
    ]
    for copy in small:
        copy.start()
    for copy in small:
        copy.wait()
    erow = lax.broadcasted_iota(jnp.int32, PT.shape[1:], 0)
    table = jnp.zeros(PT.shape[1:], jnp.float32)
    for k in range(top):
        table = table + jnp.where(ids[k : k + 1, :] == erow, probs[k : k + 1, :], 0.0)
    PT[me] = table

    arrivals = n_a + n_b - 1 + jnp.where(z > 0, 1, 0) + jnp.where(z < n_z - 1, 1, 0)
    pl.semaphore_wait(barrier, arrivals)

    full = (PT, X, G)
    own = (PT.at[me], tok, cot)

    def hop(k, d, src, mine):
        there = me + (CORES if d == 0 else -CORES)
        return pltpu.make_async_remote_copy(
            src_ref=own[k] if mine else full[k].at[src],
            dst_ref=full[k].at[src],
            send_sem=chain_s.at[k, d, src],
            recv_sem=blk_r.at[k, src],
            device_id={"expert": there},
            device_id_type=MESH,
        )

    def across(k, src, mine):
        return pltpu.make_async_remote_copy(
            src_ref=own[k] if mine else full[k].at[src],
            dst_ref=full[k].at[src],
            send_sem=sib_s.at[k, src],
            recv_sem=blk_r.at[k, src],
            device_id={"expert": sib},
            device_id_type=MESH,
        )

    def can(d):
        return z < n_z - 1 if d == 0 else z > 0

    for k in range(3):
        for d in range(2):
            @pl.when(can(d))
            def _():
                hop(k, d, me, True).start()
        across(k, me, True).start()
    local = [
        pltpu.make_async_copy(tok, X.at[me], lsem.at[0]),
        pltpu.make_async_copy(cot, G.at[me], lsem.at[1]),
        pltpu.make_async_copy(wg_in.at[0], WG, lsem.at[2]),
        pltpu.make_async_copy(wu_in.at[0], WU, lsem.at[3]),
        pltpu.make_async_copy(wd_in.at[0], WD, lsem.at[4]),
    ]
    for copy in local:
        copy.start()
    for copy in local:
        copy.wait()

    pair = CORES * rows

    def base(zz):
        return pl.multiple_of(zz * pair, pair)

    def forward_tokens(zz, d):
        for k in range(2):
            across(k, zz * CORES + (1 - c), False).wait_recv()
        x = X[pl.ds(zz * CORES, CORES)].reshape(pair, width)
        GU[d, :, :hid] = jnp.dot(x, WG[...], preferred_element_type=jnp.float32)
        GU[d, :, hid:] = jnp.dot(x, WU[...], preferred_element_type=jnp.float32)
        XT[:, pl.ds(base(zz), pair)] = x.T

    def forward_cots(zz, d):
        across(2, zz * CORES + (1 - c), False).wait_recv()
        at = base(zz)
        parts = []
        for h in range(CORES):
            p = PT[zz * CORES + h, pl.ds(me, 1), :]
            p = jnp.broadcast_to(p, (rows, rows)).T[:, :1]
            parts.append((p * G[zz * CORES + h].astype(jnp.float32)).astype(jnp.bfloat16))
        scaled = jnp.concatenate(parts, axis=0)
        S[pl.ds(at, pair), :] = scaled
        gh = lax.dot_general(scaled, WD[...], (((1,), (1,)), ((), ())), preferred_element_type=jnp.float32)
        gate, up = GU[d, :, :hid], GU[d, :, hid:]
        sigma = jax.nn.sigmoid(gate)
        active = gate * sigma
        GG[pl.ds(at, pair), :hid] = (gh * up * sigma * (1.0 + gate * (1.0 - sigma))).astype(jnp.bfloat16)
        GG[pl.ds(at, pair), hid:] = (gh * active).astype(jnp.bfloat16)
        HT[:, pl.ds(at, pair)] = (active * up).astype(jnp.bfloat16).T

    def both(s, work):
        @pl.loop(0, 2)
        def _(d):
            zz = jnp.where(d == 0, z - s, z + s)

            @pl.when((zz >= 0) & (zz < n_z) & ((s > 0) | (d == 0)))
            def _():
                work(zz, d)

    def pass_on(s, kinds):
        for k in kinds:
            for d in range(2):
                zz = z - s if d == 0 else z + s
                src = zz * CORES + c

                @pl.when((zz >= 0) & (zz < n_z))
                def _():
                    hop(k, d, src, False).wait_recv()

                    @pl.when(can(d))
                    def _():
                        hop(k, d, src, False).start()

                    across(k, src, False).start()

    @pl.loop(0, n_z)
    def _(s):
        @pl.when(s > 0)
        def _():
            pass_on(s, (0, 1))

        both(s, forward_tokens)

        @pl.when(s > 0)
        def _():
            pass_on(s, (2,))

        both(s, forward_cots)

    piece, hpiece = width // n_d, hid // n_d
    chunk = max(piece, min(256, width))
    n_c = width // chunk
    hchunk, per = hid // n_c, chunk // piece
    half = width // 2

    def index(p, second, first):
        return second * n_b + first if p == 0 else first * n_b + second

    def first_of(p, j):
        return j % n_b if p == 0 else j // n_b

    def second_of(p, j):
        return j // n_b if p == 0 else j % n_b

    def mpiece(p, j):
        return MB.at[p, pl.ds(pl.multiple_of(j * piece, piece), piece)]

    def one(p, t, j):
        mine, there = first_of(p, dd), second_of(p, j)
        return pltpu.make_async_remote_copy(
            src_ref=mpiece(p, j) if t == 0 else DB.at[p, j],
            dst_ref=(MR if t == 0 else DR).at[p, mine, there],
            send_sem=one_s.at[p, t, j],
            recv_sem=one_r.at[p, t, mine, there],
            device_id={"dp": index(p, second_of(p, dd), first_of(p, j))},
            device_id_type=MESH,
        )

    def one_from(p, t, first, second):
        dst = (MR if t == 0 else DR).at[p, first, second]
        return pltpu.make_async_remote_copy(
            src_ref=dst, dst_ref=dst,
            send_sem=one_s.at[p, t, 0],
            recv_sem=one_r.at[p, t, first, second],
            device_id={"dp": index(p, second_of(p, dd), first)},
            device_id_type=MESH,
        )

    def two(p, t, second, slot):
        return pltpu.make_async_remote_copy(
            src_ref=(MP if t == 0 else DP).at[p, second],
            dst_ref=(MQ if t == 0 else DQ).at[p, slot],
            send_sem=two_s.at[p, t, second],
            recv_sem=two_r.at[p, t, slot],
            device_id={"dp": index(p, second, first_of(p, dd))},
            device_id_type=MESH,
        )

    @pl.loop(0, n_c)
    def _(i):
        if per == 1:
            step_a, step_b = n_a - 1 - i // n_b, n_b - 1 - i % n_b
            cc = ((dd // n_b + step_a) % n_a) * n_b + (dd % n_b + step_b) % n_b
        else:
            cc = (dd // per + 1 + i) % n_c
        at = pl.multiple_of(cc * chunk, chunk)
        hat = pl.multiple_of(cc * hchunk, hchunk)
        up_gate = jnp.dot(
            XT[pl.ds(at, chunk), :], GG[...], preferred_element_type=jnp.float32
        ).astype(jnp.bfloat16)
        for p in range(2):
            MB[p, pl.ds(at, chunk), :] = up_gate[:, p * hid : (p + 1) * hid]
        for t in range(2):
            if t == 1:
                down = jnp.dot(
                    HT[pl.ds(hat, hchunk), :], S[...], preferred_element_type=jnp.float32
                ).astype(jnp.bfloat16)
                for p in range(2):
                    for q in range(per):
                        DB[p, cc * per + q] = down[q * hpiece : (q + 1) * hpiece, p * half : (p + 1) * half]
            for p in range(2):
                for q in range(per):
                    j = cc * per + q

                    @pl.when(first_of(p, j) != first_of(p, dd))
                    def _():
                        one(p, t, j).start()

    def partial(p, t, second):
        first = first_of(p, dd)
        count = n_b if p == 0 else n_a
        j = index(p, second, first)
        total = (mpiece(p, j)[...] if t == 0 else DB[p, j]).astype(jnp.float32)
        for i in range(1, count):
            other = (first + i) % count
            one_from(p, t, other, second).wait_recv()
            total = total + (MR if t == 0 else DR)[p, other, second].astype(jnp.float32)
        return total

    for t in range(2):
        for p in range(2):
            count = n_a if p == 0 else n_b

            @pl.loop(1, count)
            def _(i):
                second = (second_of(p, dd) + i) % count
                (MP if t == 0 else DP)[p, second] = partial(p, t, second).astype(jnp.bfloat16)
                two(p, t, second, second_of(p, dd)).start()

    for t in range(2):
        for p in range(2):
            count = n_a if p == 0 else n_b
            mine = second_of(p, dd)
            total = partial(p, t, mine)
            for i in range(1, count):
                other = (mine + i) % count
                two(p, t, other, other).wait_recv()
                total = total + (MQ if t == 0 else DQ)[p, other].astype(jnp.float32)
            if t == 0:
                (out_g, out_u)[p][0] = total.astype(jnp.bfloat16)
            else:
                out_d[0, :, p * half : (p + 1) * half] = total.astype(jnp.bfloat16)

    for p in range(2):
        for t in range(2):
            @pl.loop(0, n_d)
            def _(j):
                @pl.when(first_of(p, j) != first_of(p, dd))
                def _():
                    one(p, t, j).wait_send()

            count = n_a if p == 0 else n_b

            @pl.loop(1, count)
            def _(i):
                two(p, t, (second_of(p, dd) + i) % count, second_of(p, dd)).wait_send()

    @pl.loop(0, n_z)
    def _(s):
        for k in range(3):
            for d in range(2):
                zz = z - s if d == 0 else z + s
                src = zz * CORES + c

                @pl.when((zz >= 0) & (zz < n_z) & can(d))
                def _():
                    hop(k, d, src, False).wait_send()

            across(k, s * CORES + c, False).wait_send()


def copy_out(*refs):
    n = len(refs) // 2
    copies = [pltpu.make_async_copy(refs[i], refs[n + i], refs[-1].at[i]) for i in range(n)]
    for copy in copies:
        copy.start()
    for copy in copies:
        copy.wait()


def write_out(arrays):
    anywhere = pl.BlockSpec(memory_space=pl.ANY)
    return pl.pallas_call(
        copy_out,
        out_shape=tuple(jax.ShapeDtypeStruct(x.shape, x.dtype) for x in arrays),
        in_specs=[anywhere] * len(arrays),
        out_specs=(anywhere,) * len(arrays),
        scratch_shapes=[pltpu.SemaphoreType.DMA((len(arrays),))],
        compiler_params=pltpu.CompilerParams(vmem_limit_bytes=1 << 20),
    )(*arrays)


def solution(mesh):
    n_e, n_d = mesh.shape["expert"], mesh.shape["dp"]
    n_b = max(b for b in range(1, n_d + 1) if n_d % b == 0 and b * b <= n_d)
    n_a = n_d // n_b

    def step(tokens, out_grad, expert_ids, gate_probs, w_gate, w_up, w_down):
        rows, width = tokens.shape
        hid = w_gate.shape[2]
        total = n_e * rows
        lanes = -(-n_e // 8) * 8
        bf, f32 = jnp.bfloat16, jnp.float32
        vmem = pl.BlockSpec(memory_space=pltpu.VMEM)
        hbm = pl.BlockSpec(memory_space=pltpu.HBM)
        piece, hpiece = width // n_d, hid // n_d
        dma = pltpu.SemaphoreType.DMA
        scratch = [
            (expert_ids.shape[::-1], expert_ids.dtype),
            (gate_probs.shape[::-1], gate_probs.dtype),
            ((n_e, rows, width), bf),
            ((n_e, rows, width), bf),
            ((n_e, lanes, rows), f32),
            ((width, hid), bf),
            ((width, hid), bf),
            ((hid, width), bf),
            ((2, CORES * rows, 2 * hid), f32),
            ((width, total), bf),
            ((hid, total), bf),
            ((total, 2 * hid), bf),
            ((total, width), bf),
            ((2, width, hid), bf),
            ((2, n_d, hpiece, width // 2), bf),
            ((2, n_a, n_a, piece, hid), bf),
            ((2, n_a, n_a, hpiece, width // 2), bf),
            ((2, n_a, piece, hid), bf),
            ((2, n_a, hpiece, width // 2), bf),
            ((2, n_a, piece, hid), bf),
            ((2, n_a, hpiece, width // 2), bf),
        ]
        held = sum(math.prod(shape) * jnp.dtype(kind).itemsize for shape, kind in scratch)
        args = (tokens, out_grad, expert_ids.T, gate_probs.T, w_gate, w_up, w_down)
        made = pl.pallas_call(
            functools.partial(kernel, n_e, n_a, n_b),
            out_shape=(
                jax.ShapeDtypeStruct((1, piece, hid), bf),
                jax.ShapeDtypeStruct((1, piece, hid), bf),
                jax.ShapeDtypeStruct((1, hpiece, width), bf),
            ),
            in_specs=[hbm] * 7,
            out_specs=(vmem, vmem, vmem),
            scratch_shapes=[pltpu.VMEM(shape, kind) for shape, kind in scratch]
            + [
                dma((7,)),
                dma((3, 2, n_e)),
                dma((3, n_e)),
                dma((3, n_e)),
                dma((2, 2, n_d)),
                dma((2, 2, n_a, n_a)),
                dma((2, 2, n_a)),
                dma((2, 2, n_a)),
            ],
            compiler_params=pltpu.CompilerParams(
                collective_id=0, has_side_effects=True, vmem_limit_bytes=held + (10 << 20)
            ),
        )(*(pltpu.with_memory_space_constraint(x, pltpu.HBM) for x in args))
        return write_out(made)

    spread = P(("expert", "dp"), None)
    return jax.shard_map(
        step,
        mesh=mesh,
        in_specs=(spread, spread, spread, spread) + (P("expert", None, None),) * 3,
        out_specs=(P("expert", "dp", None),) * 3,
        check_vma=False,
    )
```

```python
import functools
import math

import jax
import jax.numpy as jnp
from jax import lax
from jax.experimental import pallas as pl
from jax.experimental.pallas import tpu as pltpu
from jax.sharding import PartitionSpec as P

MESH = pl.DeviceIdType.MESH
CORES = 2
QUARTERS = 4


def kernel(
    n_e, n_a, n_b,
    tok, cot, ids_in, probs_in, wg_in, wu_in, wd_in,
    out_g, out_u, out_d,
    ids, probs, X, G, PT, WG, WU, WD, GU, GH, XT, HT, GG, S, MB, DB, MR, DR, MP, DP, MQ, DQ,
    lsem, chain_s, sib_s, blk_r, one_s, one_r, two_s, two_r,
):
    n_d = n_a * n_b
    rows, width = tok.shape
    hid = wg_in.shape[2]
    top = ids_in.shape[0]
    n_z = n_e // CORES
    me = lax.axis_index("expert")
    dd = lax.axis_index("dp")
    z, c = me // CORES, me % CORES
    sib = z * CORES + (1 - c)

    barrier = pltpu.get_barrier_semaphore()
    for step in (-1, 1):
        @pl.when(jnp.logical_and(z + step >= 0, z + step < n_z))
        def _():
            pl.semaphore_signal(barrier, inc=1, device_id={"expert": me + step * CORES}, device_id_type=MESH)
    pl.semaphore_signal(barrier, inc=1, device_id={"expert": sib}, device_id_type=MESH)
    for i in range(1, n_a):
        pl.semaphore_signal(barrier, inc=1, device_id={"dp": ((dd // n_b + i) % n_a) * n_b + dd % n_b}, device_id_type=MESH)
    for i in range(1, n_b):
        pl.semaphore_signal(barrier, inc=1, device_id={"dp": dd // n_b * n_b + (dd % n_b + i) % n_b}, device_id_type=MESH)
    small = [
        pltpu.make_async_copy(ids_in, ids, lsem.at[5]),
        pltpu.make_async_copy(probs_in, probs, lsem.at[6]),
    ]
    for copy in small:
        copy.start()
    for copy in small:
        copy.wait()
    erow = lax.broadcasted_iota(jnp.int32, PT.shape[1:], 0)
    table = jnp.zeros(PT.shape[1:], jnp.float32)
    for k in range(top):
        table = table + jnp.where(ids[k : k + 1, :] == erow, probs[k : k + 1, :], 0.0)
    PT[me] = table

    arrivals = n_a + n_b - 1 + jnp.where(z > 0, 1, 0) + jnp.where(z < n_z - 1, 1, 0)
    pl.semaphore_wait(barrier, arrivals)

    wide = width // QUARTERS

    def full(k, src):
        if k < 2:
            return (PT, X)[k].at[src]
        return G.at[src, :, pl.ds((k - 2) * wide, wide)]

    def own(k):
        if k < 2:
            return (PT.at[me], tok)[k]
        return cot.at[:, pl.ds((k - 2) * wide, wide)]

    def hop(k, d, src, mine):
        there = me + (CORES if d == 0 else -CORES)
        return pltpu.make_async_remote_copy(
            src_ref=own(k) if mine else full(k, src),
            dst_ref=full(k, src),
            send_sem=chain_s.at[k, d, src],
            recv_sem=blk_r.at[k, src],
            device_id={"expert": there},
            device_id_type=MESH,
        )

    def across(k, src, mine):
        return pltpu.make_async_remote_copy(
            src_ref=own(k) if mine else full(k, src),
            dst_ref=full(k, src),
            send_sem=sib_s.at[k, src],
            recv_sem=blk_r.at[k, src],
            device_id={"expert": sib},
            device_id_type=MESH,
        )

    def can(d):
        return z < n_z - 1 if d == 0 else z > 0

    kinds = 2 + QUARTERS
    for k in range(kinds):
        for d in range(2):
            @pl.when(can(d) if k < 2 else z == (0 if d == 0 else n_z - 1))
            def _():
                hop(k, d, me, True).start()
        across(k, me, True).start()
    local = [
        pltpu.make_async_copy(tok, X.at[me], lsem.at[0]),
        pltpu.make_async_copy(cot, G.at[me], lsem.at[1]),
        pltpu.make_async_copy(wg_in.at[0], WG, lsem.at[2]),
        pltpu.make_async_copy(wu_in.at[0], WU, lsem.at[3]),
        pltpu.make_async_copy(wd_in.at[0], WD, lsem.at[4]),
    ]
    for copy in local:
        copy.start()
    for copy in local:
        copy.wait()

    pair = CORES * rows

    def base(zz):
        return pl.multiple_of(zz * pair, pair)

    def forward_tokens(zz):
        for k in range(2):
            across(k, zz * CORES + (1 - c), False).wait_recv()
        at = base(zz)
        x = X[pl.ds(zz * CORES, CORES)].reshape(pair, width)
        gate = jnp.dot(x, WG[...], preferred_element_type=jnp.float32)
        up = jnp.dot(x, WU[...], preferred_element_type=jnp.float32)
        sigma = jax.nn.sigmoid(gate)
        active = gate * sigma
        GU[pl.ds(at, pair), :hid] = up * sigma * (1.0 + gate * (1.0 - sigma))
        GU[pl.ds(at, pair), hid:] = active
        HT[:, pl.ds(at, pair)] = (active * up).astype(jnp.bfloat16).T
        XT[:, pl.ds(at, pair)] = x.T

    def forward_cots(zz, q):
        across(2 + q, zz * CORES + (1 - c), False).wait_recv()
        at = base(zz)
        cols = slice(q * wide, (q + 1) * wide)
        parts = []
        for h in range(CORES):
            p = PT[zz * CORES + h, pl.ds(me, 1), :]
            p = jnp.broadcast_to(p, (rows, rows)).T[:, :1]
            parts.append((p * G[zz * CORES + h, :, cols].astype(jnp.float32)).astype(jnp.bfloat16))
        scaled = jnp.concatenate(parts, axis=0)
        S[pl.ds(at, pair), cols] = scaled
        gh = lax.dot_general(scaled, WD[:, cols], (((1,), (1,)), ((), ())), preferred_element_type=jnp.float32)
        if q > 0:
            gh = gh + GH[pl.ds(at, pair), :]
        if q < QUARTERS - 1:
            GH[pl.ds(at, pair), :] = gh
        else:
            GG[pl.ds(at, pair), :hid] = (gh * GU[pl.ds(at, pair), :hid]).astype(jnp.bfloat16)
            GG[pl.ds(at, pair), hid:] = (gh * GU[pl.ds(at, pair), hid:]).astype(jnp.bfloat16)

    def both(s, work):
        @pl.loop(0, 2)
        def _(d):
            zz = jnp.where(d == 0, z - s, z + s)

            @pl.when((zz >= 0) & (zz < n_z) & ((s > 0) | (d == 0)))
            def _():
                work(zz)

    def pass_on(s, group, after):
        for k in group:
            for d in range(2):
                zz = z - s if d == 0 else z + s
                src = zz * CORES + c

                @pl.when((zz >= 0) & (zz < n_z))
                def _():
                    hop(k, d, src, False).wait_recv()

                    @pl.when(can(d))
                    def _():
                        hop(k, d, src, False).start()

                    across(k, src, False).start()

                if k == group[-1] and after < kinds:
                    @pl.when((zz == (0 if d == 0 else n_z - 1)) & can(d))
                    def _():
                        hop(after, d, me, True).start()

    @pl.loop(0, n_z)
    def _(s):
        @pl.when(s > 0)
        def _():
            pass_on(s, (0, 1), 2)

        both(s, forward_tokens)

    piece, hpiece = width // n_d, hid // n_d
    chunk = max(piece, min(256, width))
    n_c = width // chunk
    hchunk, per = hid // n_c, chunk // piece

    def index(p, second, first):
        return second * n_b + first if p == 0 else first * n_b + second

    def first_of(p, j):
        return j % n_b if p == 0 else j // n_b

    def second_of(p, j):
        return j // n_b if p == 0 else j % n_b

    def mpiece(p, j):
        return MB.at[p, pl.ds(pl.multiple_of(j * piece, piece), piece)]

    def path(t):
        return t % 2

    def buffers(t):
        return (MR.at[t], MP.at[t], MQ.at[t]) if t < 2 else (DR.at[t - 2], DP.at[t - 2], DQ.at[t - 2])

    def source(t, j):
        return mpiece(t, j) if t < 2 else DB.at[t - 2, j]

    def one(t, j):
        p = path(t)
        mine, there = first_of(p, dd), second_of(p, j)
        return pltpu.make_async_remote_copy(
            src_ref=source(t, j),
            dst_ref=buffers(t)[0].at[mine, there],
            send_sem=one_s.at[t, j],
            recv_sem=one_r.at[t, mine, there],
            device_id={"dp": index(p, second_of(p, dd), first_of(p, j))},
            device_id_type=MESH,
        )

    def one_from(t, first, second):
        dst = buffers(t)[0].at[first, second]
        return pltpu.make_async_remote_copy(
            src_ref=dst, dst_ref=dst,
            send_sem=one_s.at[t, 0],
            recv_sem=one_r.at[t, first, second],
            device_id={"dp": index(path(t), second_of(path(t), dd), first)},
            device_id_type=MESH,
        )

    def two(t, second, slot):
        p = path(t)
        return pltpu.make_async_remote_copy(
            src_ref=buffers(t)[1].at[second],
            dst_ref=buffers(t)[2].at[slot],
            send_sem=two_s.at[t, second],
            recv_sem=two_r.at[t, slot],
            device_id={"dp": index(p, second, first_of(p, dd))},
            device_id_type=MESH,
        )

    def partial(t, second):
        p = path(t)
        first = first_of(p, dd)
        count = n_b if p == 0 else n_a
        total = source(t, index(p, second, first))[...].astype(jnp.float32)
        for i in range(1, count):
            other = (first + i) % count
            one_from(t, other, second).wait_recv()
            total = total + buffers(t)[0][other, second].astype(jnp.float32)
        return total

    def seconds(t):
        return n_a if path(t) == 0 else n_b

    def relay(t):
        @pl.loop(1, seconds(t))
        def _(i):
            second = (second_of(path(t), dd) + i) % seconds(t)
            buffers(t)[1][second] = partial(t, second).astype(jnp.bfloat16)
            two(t, second, second_of(path(t), dd)).start()

    def turn(i):
        if per == 1:
            step_a, step_b = n_a - 1 - i // n_b, n_b - 1 - i % n_b
            return ((dd // n_b + step_a) % n_a) * n_b + (dd % n_b + step_b) % n_b
        return (dd // per + 1 + i) % n_c

    def give(t, j):
        @pl.when(first_of(path(t), j) != first_of(path(t), dd))
        def _():
            one(t, j).start()

    def make_down(q):
        @pl.loop(0, n_c)
        def _(i):
            cc = turn(i)
            hat = pl.multiple_of(cc * hchunk, hchunk)
            down = jnp.dot(
                HT[pl.ds(hat, hchunk), :], S[:, q * wide : (q + 1) * wide], preferred_element_type=jnp.float32
            ).astype(jnp.bfloat16)
            for r in range(per):
                DB[q, cc * per + r] = down[r * hpiece : (r + 1) * hpiece]
            for r in range(per):
                give(2 + q, cc * per + r)

    for q in range(QUARTERS):
        @pl.loop(0, n_z)
        def _(s):
            @pl.when(s > 0)
            def _():
                pass_on(s, (2 + q,), 3 + q)

            both(s, functools.partial(forward_cots, q=q))

        if q < QUARTERS - 1:
            make_down(q)
        if q > 0:
            relay(1 + q)

    @pl.loop(0, n_c)
    def _(i):
        cc = turn(i)
        at = pl.multiple_of(cc * chunk, chunk)
        both_grads = jnp.dot(
            XT[pl.ds(at, chunk), :], GG[...], preferred_element_type=jnp.float32
        ).astype(jnp.bfloat16)
        for t in range(2):
            MB[t, pl.ds(at, chunk), :] = both_grads[:, t * hid : (t + 1) * hid]
        for t in range(2):
            for r in range(per):
                give(t, cc * per + r)

    make_down(QUARTERS - 1)
    for t in (0, 1, 1 + QUARTERS):
        relay(t)

    for t in tuple(range(2, 1 + QUARTERS)) + (0, 1, 1 + QUARTERS):
        mine = second_of(path(t), dd)
        total = partial(t, mine)
        for i in range(1, seconds(t)):
            other = (mine + i) % seconds(t)
            two(t, other, other).wait_recv()
            total = total + buffers(t)[2][other].astype(jnp.float32)
        if t < 2:
            (out_g, out_u)[t][0] = total.astype(jnp.bfloat16)
        else:
            out_d[0, :, (t - 2) * wide : (t - 1) * wide] = total.astype(jnp.bfloat16)

    for t in range(2 + QUARTERS):
        @pl.loop(0, n_d)
        def _(j):
            @pl.when(first_of(path(t), j) != first_of(path(t), dd))
            def _():
                one(t, j).wait_send()

        @pl.loop(1, seconds(t))
        def _(i):
            two(t, (second_of(path(t), dd) + i) % seconds(t), second_of(path(t), dd)).wait_send()

    @pl.loop(0, n_z)
    def _(s):
        for k in range(kinds):
            for d in range(2):
                zz = z - s if d == 0 else z + s
                src = zz * CORES + c

                @pl.when((zz >= 0) & (zz < n_z) & can(d))
                def _():
                    hop(k, d, src, False).wait_send()

            across(k, s * CORES + c, False).wait_send()


def copy_out(*refs):
    n = len(refs) // 2
    copies = [pltpu.make_async_copy(refs[i], refs[n + i], refs[-1].at[i]) for i in range(n)]
    for copy in copies:
        copy.start()
    for copy in copies:
        copy.wait()


def write_out(arrays):
    anywhere = pl.BlockSpec(memory_space=pl.ANY)
    return pl.pallas_call(
        copy_out,
        out_shape=tuple(jax.ShapeDtypeStruct(x.shape, x.dtype) for x in arrays),
        in_specs=[anywhere] * len(arrays),
        out_specs=(anywhere,) * len(arrays),
        scratch_shapes=[pltpu.SemaphoreType.DMA((len(arrays),))],
        compiler_params=pltpu.CompilerParams(vmem_limit_bytes=1 << 20),
    )(*arrays)


def solution(mesh):
    n_e, n_d = mesh.shape["expert"], mesh.shape["dp"]
    n_b = max(b for b in range(1, n_d + 1) if n_d % b == 0 and b * b <= n_d)
    n_a = n_d // n_b

    def step(tokens, out_grad, expert_ids, gate_probs, w_gate, w_up, w_down):
        rows, width = tokens.shape
        hid = w_gate.shape[2]
        total = n_e * rows
        lanes = -(-n_e // 8) * 8
        bf, f32 = jnp.bfloat16, jnp.float32
        vmem = pl.BlockSpec(memory_space=pltpu.VMEM)
        hbm = pl.BlockSpec(memory_space=pltpu.HBM)
        piece, hpiece = width // n_d, hid // n_d
        dma = pltpu.SemaphoreType.DMA
        scratch = [
            (expert_ids.shape[::-1], expert_ids.dtype),
            (gate_probs.shape[::-1], gate_probs.dtype),
            ((n_e, rows, width), bf),
            ((n_e, rows, width), bf),
            ((n_e, lanes, rows), f32),
            ((width, hid), bf),
            ((width, hid), bf),
            ((hid, width), bf),
            ((total, 2 * hid), f32),
            ((total, hid), f32),
            ((width, total), bf),
            ((hid, total), bf),
            ((total, 2 * hid), bf),
            ((total, width), bf),
            ((2, width, hid), bf),
            ((QUARTERS, n_d, hpiece, width // QUARTERS), bf),
            ((2, n_a, n_a, piece, hid), bf),
            ((QUARTERS, n_a, n_a, hpiece, width // QUARTERS), bf),
            ((2, n_a, piece, hid), bf),
            ((QUARTERS, n_a, hpiece, width // QUARTERS), bf),
            ((2, n_a, piece, hid), bf),
            ((QUARTERS, n_a, hpiece, width // QUARTERS), bf),
        ]
        held = sum(math.prod(shape) * jnp.dtype(kind).itemsize for shape, kind in scratch)
        args = (tokens, out_grad, expert_ids.T, gate_probs.T, w_gate, w_up, w_down)
        made = pl.pallas_call(
            functools.partial(kernel, n_e, n_a, n_b),
            out_shape=(
                jax.ShapeDtypeStruct((1, piece, hid), bf),
                jax.ShapeDtypeStruct((1, piece, hid), bf),
                jax.ShapeDtypeStruct((1, hpiece, width), bf),
            ),
            in_specs=[hbm] * 7,
            out_specs=(vmem, vmem, vmem),
            scratch_shapes=[pltpu.VMEM(shape, kind) for shape, kind in scratch]
            + [
                dma((7,)),
                dma((2 + QUARTERS, 2, n_e)),
                dma((2 + QUARTERS, n_e)),
                dma((2 + QUARTERS, n_e)),
                dma((2 + QUARTERS, n_d)),
                dma((2 + QUARTERS, n_a, n_a)),
                dma((2 + QUARTERS, n_a)),
                dma((2 + QUARTERS, n_a)),
            ],
            compiler_params=pltpu.CompilerParams(
                collective_id=0, has_side_effects=True, vmem_limit_bytes=held + (10 << 20)
            ),
        )(*(pltpu.with_memory_space_constraint(x, pltpu.HBM) for x in args))
        return write_out(made)

    spread = P(("expert", "dp"), None)
    return jax.shard_map(
        step,
        mesh=mesh,
        in_specs=(spread, spread, spread, spread) + (P("expert", None, None),) * 3,
        out_specs=(P("expert", "dp", None),) * 3,
        check_vma=False,
    )
```

```python
import functools
import math

import jax
import jax.numpy as jnp
from jax import lax
from jax.experimental import pallas as pl
from jax.experimental.pallas import tpu as pltpu
from jax.sharding import PartitionSpec as P

MESH = pl.DeviceIdType.MESH
CORES = 2
QUARTERS = 2


def kernel(
    n_e, n_a, n_b,
    tok, cot, ids_in, probs_in, wg_in, wu_in, wd_in,
    out_g, out_u, out_d,
    ids, probs, X, G, PT, WG, WU, WD, GU, GH, XT, HT, GG, S, MB, DB, MR, DR, MP, DP, MQ, DQ,
    lsem, chain_s, sib_s, blk_r, one_s, one_r, two_s, two_r,
):
    n_d = n_a * n_b
    rows, width = tok.shape
    hid = wg_in.shape[2]
    top = ids_in.shape[0]
    n_z = n_e // CORES
    me = lax.axis_index("expert")
    dd = lax.axis_index("dp")
    z, c = me // CORES, me % CORES
    sib = z * CORES + (1 - c)

    barrier = pltpu.get_barrier_semaphore()
    for step in (-1, 1):
        @pl.when(jnp.logical_and(z + step >= 0, z + step < n_z))
        def _():
            pl.semaphore_signal(barrier, inc=1, device_id={"expert": me + step * CORES}, device_id_type=MESH)
    pl.semaphore_signal(barrier, inc=1, device_id={"expert": sib}, device_id_type=MESH)
    for i in range(1, n_a):
        pl.semaphore_signal(barrier, inc=1, device_id={"dp": ((dd // n_b + i) % n_a) * n_b + dd % n_b}, device_id_type=MESH)
    for i in range(1, n_b):
        pl.semaphore_signal(barrier, inc=1, device_id={"dp": dd // n_b * n_b + (dd % n_b + i) % n_b}, device_id_type=MESH)
    small = [
        pltpu.make_async_copy(ids_in, ids, lsem.at[5]),
        pltpu.make_async_copy(probs_in, probs, lsem.at[6]),
    ]
    for copy in small:
        copy.start()
    for copy in small:
        copy.wait()
    erow = lax.broadcasted_iota(jnp.int32, PT.shape[1:], 0)
    table = jnp.zeros(PT.shape[1:], jnp.float32)
    for k in range(top):
        table = table + jnp.where(ids[k : k + 1, :] == erow, probs[k : k + 1, :], 0.0)
    PT[me] = table

    arrivals = n_a + n_b - 1 + jnp.where(z > 0, 1, 0) + jnp.where(z < n_z - 1, 1, 0)
    pl.semaphore_wait(barrier, arrivals)

    wide = width // QUARTERS

    def full(k, src):
        if k < 2:
            return (PT, X)[k].at[src]
        return G.at[src, :, pl.ds((k - 2) * wide, wide)]

    def own(k):
        if k < 2:
            return (PT.at[me], tok)[k]
        return cot.at[:, pl.ds((k - 2) * wide, wide)]

    def hop(k, d, src, mine):
        there = me + (CORES if d == 0 else -CORES)
        return pltpu.make_async_remote_copy(
            src_ref=own(k) if mine else full(k, src),
            dst_ref=full(k, src),
            send_sem=chain_s.at[k, d, src],
            recv_sem=blk_r.at[k, src],
            device_id={"expert": there},
            device_id_type=MESH,
        )

    def across(k, src, mine):
        return pltpu.make_async_remote_copy(
            src_ref=own(k) if mine else full(k, src),
            dst_ref=full(k, src),
            send_sem=sib_s.at[k, src],
            recv_sem=blk_r.at[k, src],
            device_id={"expert": sib},
            device_id_type=MESH,
        )

    def can(d):
        return z < n_z - 1 if d == 0 else z > 0

    kinds = 2 + QUARTERS
    for k in range(kinds):
        for d in range(2):
            @pl.when(can(d) if k < 2 else z == (0 if d == 0 else n_z - 1))
            def _():
                hop(k, d, me, True).start()
        across(k, me, True).start()
    local = [
        pltpu.make_async_copy(tok, X.at[me], lsem.at[0]),
        pltpu.make_async_copy(cot, G.at[me], lsem.at[1]),
        pltpu.make_async_copy(wg_in.at[0], WG, lsem.at[2]),
        pltpu.make_async_copy(wu_in.at[0], WU, lsem.at[3]),
        pltpu.make_async_copy(wd_in.at[0], WD, lsem.at[4]),
    ]
    for copy in local:
        copy.start()
    for copy in local:
        copy.wait()

    pair = CORES * rows

    def base(zz):
        return pl.multiple_of(zz * pair, pair)

    def forward_tokens(zz):
        for k in range(2):
            across(k, zz * CORES + (1 - c), False).wait_recv()
        at = base(zz)
        x = X[pl.ds(zz * CORES, CORES)].reshape(pair, width)
        gate = jnp.dot(x, WG[...], preferred_element_type=jnp.float32)
        up = jnp.dot(x, WU[...], preferred_element_type=jnp.float32)
        sigma = jax.nn.sigmoid(gate)
        active = gate * sigma
        GU[pl.ds(at, pair), :hid] = up * sigma * (1.0 + gate * (1.0 - sigma))
        GU[pl.ds(at, pair), hid:] = active
        HT[:, pl.ds(at, pair)] = (active * up).astype(jnp.bfloat16).T
        XT[:, pl.ds(at, pair)] = x.T

    def forward_cots(zz, q):
        across(2 + q, zz * CORES + (1 - c), False).wait_recv()
        at = base(zz)
        cols = slice(q * wide, (q + 1) * wide)
        parts = []
        for h in range(CORES):
            p = PT[zz * CORES + h, pl.ds(me, 1), :]
            p = jnp.broadcast_to(p, (rows, rows)).T[:, :1]
            parts.append((p * G[zz * CORES + h, :, cols].astype(jnp.float32)).astype(jnp.bfloat16))
        scaled = jnp.concatenate(parts, axis=0)
        S[pl.ds(at, pair), cols] = scaled
        gh = lax.dot_general(scaled, WD[:, cols], (((1,), (1,)), ((), ())), preferred_element_type=jnp.float32)
        if q > 0:
            gh = gh + GH[pl.ds(at, pair), :]
        if q < QUARTERS - 1:
            GH[pl.ds(at, pair), :] = gh
        else:
            GG[pl.ds(at, pair), :hid] = (gh * GU[pl.ds(at, pair), :hid]).astype(jnp.bfloat16)
            GG[pl.ds(at, pair), hid:] = (gh * GU[pl.ds(at, pair), hid:]).astype(jnp.bfloat16)

    def both(s, work):
        @pl.loop(0, 2)
        def _(d):
            zz = jnp.where(d == 0, z - s, z + s)

            @pl.when((zz >= 0) & (zz < n_z) & ((s > 0) | (d == 0)))
            def _():
                work(zz)

    def pass_on(s, group, after):
        for k in group:
            for d in range(2):
                zz = z - s if d == 0 else z + s
                src = zz * CORES + c

                @pl.when((zz >= 0) & (zz < n_z))
                def _():
                    hop(k, d, src, False).wait_recv()

                    @pl.when(can(d))
                    def _():
                        hop(k, d, src, False).start()

                    across(k, src, False).start()

                if k == group[-1] and after < kinds:
                    @pl.when((zz == (0 if d == 0 else n_z - 1)) & can(d))
                    def _():
                        hop(after, d, me, True).start()

    @pl.loop(0, n_z)
    def _(s):
        @pl.when(s > 0)
        def _():
            pass_on(s, (0, 1), 2)

        both(s, forward_tokens)

    piece, hpiece = width // n_d, hid // n_d
    chunk = max(piece, min(256, width))
    n_c = width // chunk
    hchunk, per = hid // n_c, chunk // piece

    def index(p, second, first):
        return second * n_b + first if p == 0 else first * n_b + second

    def first_of(p, j):
        return j % n_b if p == 0 else j // n_b

    def second_of(p, j):
        return j // n_b if p == 0 else j % n_b

    def mpiece(p, j):
        return MB.at[p, pl.ds(pl.multiple_of(j * piece, piece), piece)]

    def path(t):
        return t % 2

    def buffers(t):
        return (MR.at[t], MP.at[t], MQ.at[t]) if t < 2 else (DR.at[t - 2], DP.at[t - 2], DQ.at[t - 2])

    def source(t, j):
        return mpiece(t, j) if t < 2 else DB.at[t - 2, j]

    def one(t, j):
        p = path(t)
        mine, there = first_of(p, dd), second_of(p, j)
        return pltpu.make_async_remote_copy(
            src_ref=source(t, j),
            dst_ref=buffers(t)[0].at[mine, there],
            send_sem=one_s.at[t, j],
            recv_sem=one_r.at[t, mine, there],
            device_id={"dp": index(p, second_of(p, dd), first_of(p, j))},
            device_id_type=MESH,
        )

    def one_from(t, first, second):
        dst = buffers(t)[0].at[first, second]
        return pltpu.make_async_remote_copy(
            src_ref=dst, dst_ref=dst,
            send_sem=one_s.at[t, 0],
            recv_sem=one_r.at[t, first, second],
            device_id={"dp": index(path(t), second_of(path(t), dd), first)},
            device_id_type=MESH,
        )

    def two(t, second, slot):
        p = path(t)
        return pltpu.make_async_remote_copy(
            src_ref=buffers(t)[1].at[second],
            dst_ref=buffers(t)[2].at[slot],
            send_sem=two_s.at[t, second],
            recv_sem=two_r.at[t, slot],
            device_id={"dp": index(p, second, first_of(p, dd))},
            device_id_type=MESH,
        )

    def partial(t, second):
        p = path(t)
        first = first_of(p, dd)
        count = n_b if p == 0 else n_a
        total = source(t, index(p, second, first))[...].astype(jnp.float32)
        for i in range(1, count):
            other = (first + i) % count
            one_from(t, other, second).wait_recv()
            total = total + buffers(t)[0][other, second].astype(jnp.float32)
        return total

    def seconds(t):
        return n_a if path(t) == 0 else n_b

    def relay(t):
        @pl.loop(1, seconds(t))
        def _(i):
            second = (second_of(path(t), dd) + i) % seconds(t)
            buffers(t)[1][second] = partial(t, second).astype(jnp.bfloat16)
            two(t, second, second_of(path(t), dd)).start()

    def turn(i):
        if per == 1:
            step_a, step_b = n_a - 1 - i // n_b, n_b - 1 - i % n_b
            return ((dd // n_b + step_a) % n_a) * n_b + (dd % n_b + step_b) % n_b
        return (dd // per + 1 + i) % n_c

    def give(t, j):
        @pl.when(first_of(path(t), j) != first_of(path(t), dd))
        def _():
            one(t, j).start()

    def make_down(q):
        @pl.loop(0, n_c)
        def _(i):
            cc = turn(i)
            hat = pl.multiple_of(cc * hchunk, hchunk)
            down = jnp.dot(
                HT[pl.ds(hat, hchunk), :], S[:, q * wide : (q + 1) * wide], preferred_element_type=jnp.float32
            ).astype(jnp.bfloat16)
            for r in range(per):
                DB[q, cc * per + r] = down[r * hpiece : (r + 1) * hpiece]
            for r in range(per):
                give(2 + q, cc * per + r)

    for q in range(QUARTERS):
        @pl.loop(0, n_z)
        def _(s):
            @pl.when(s > 0)
            def _():
                pass_on(s, (2 + q,), 3 + q)

            both(s, functools.partial(forward_cots, q=q))

        if q < QUARTERS - 1:
            make_down(q)
        if q > 0:
            relay(1 + q)

    @pl.loop(0, n_c)
    def _(i):
        cc = turn(i)
        at = pl.multiple_of(cc * chunk, chunk)
        both_grads = jnp.dot(
            XT[pl.ds(at, chunk), :], GG[...], preferred_element_type=jnp.float32
        ).astype(jnp.bfloat16)
        for t in range(2):
            MB[t, pl.ds(at, chunk), :] = both_grads[:, t * hid : (t + 1) * hid]
        for t in range(2):
            for r in range(per):
                give(t, cc * per + r)

    make_down(QUARTERS - 1)
    for t in (0, 1, 1 + QUARTERS):
        relay(t)

    for t in tuple(range(2, 1 + QUARTERS)) + (0, 1, 1 + QUARTERS):
        mine = second_of(path(t), dd)
        total = partial(t, mine)
        for i in range(1, seconds(t)):
            other = (mine + i) % seconds(t)
            two(t, other, other).wait_recv()
            total = total + buffers(t)[2][other].astype(jnp.float32)
        if t < 2:
            (out_g, out_u)[t][0] = total.astype(jnp.bfloat16)
        else:
            out_d[0, :, (t - 2) * wide : (t - 1) * wide] = total.astype(jnp.bfloat16)

    for t in range(2 + QUARTERS):
        @pl.loop(0, n_d)
        def _(j):
            @pl.when(first_of(path(t), j) != first_of(path(t), dd))
            def _():
                one(t, j).wait_send()

        @pl.loop(1, seconds(t))
        def _(i):
            two(t, (second_of(path(t), dd) + i) % seconds(t), second_of(path(t), dd)).wait_send()

    @pl.loop(0, n_z)
    def _(s):
        for k in range(kinds):
            for d in range(2):
                zz = z - s if d == 0 else z + s
                src = zz * CORES + c

                @pl.when((zz >= 0) & (zz < n_z) & can(d))
                def _():
                    hop(k, d, src, False).wait_send()

            across(k, s * CORES + c, False).wait_send()


def copy_out(*refs):
    n = len(refs) // 2
    copies = [pltpu.make_async_copy(refs[i], refs[n + i], refs[-1].at[i]) for i in range(n)]
    for copy in copies:
        copy.start()
    for copy in copies:
        copy.wait()


def write_out(arrays):
    anywhere = pl.BlockSpec(memory_space=pl.ANY)
    return pl.pallas_call(
        copy_out,
        out_shape=tuple(jax.ShapeDtypeStruct(x.shape, x.dtype) for x in arrays),
        in_specs=[anywhere] * len(arrays),
        out_specs=(anywhere,) * len(arrays),
        scratch_shapes=[pltpu.SemaphoreType.DMA((len(arrays),))],
        compiler_params=pltpu.CompilerParams(vmem_limit_bytes=1 << 20),
    )(*arrays)


def solution(mesh):
    n_e, n_d = mesh.shape["expert"], mesh.shape["dp"]
    n_b = max(b for b in range(1, n_d + 1) if n_d % b == 0 and b * b <= n_d)
    n_a = n_d // n_b

    def step(tokens, out_grad, expert_ids, gate_probs, w_gate, w_up, w_down):
        rows, width = tokens.shape
        hid = w_gate.shape[2]
        total = n_e * rows
        lanes = -(-n_e // 8) * 8
        bf, f32 = jnp.bfloat16, jnp.float32
        vmem = pl.BlockSpec(memory_space=pltpu.VMEM)
        hbm = pl.BlockSpec(memory_space=pltpu.HBM)
        piece, hpiece = width // n_d, hid // n_d
        dma = pltpu.SemaphoreType.DMA
        scratch = [
            (expert_ids.shape[::-1], expert_ids.dtype),
            (gate_probs.shape[::-1], gate_probs.dtype),
            ((n_e, rows, width), bf),
            ((n_e, rows, width), bf),
            ((n_e, lanes, rows), f32),
            ((width, hid), bf),
            ((width, hid), bf),
            ((hid, width), bf),
            ((total, 2 * hid), f32),
            ((total, hid), f32),
            ((width, total), bf),
            ((hid, total), bf),
            ((total, 2 * hid), bf),
            ((total, width), bf),
            ((2, width, hid), bf),
            ((QUARTERS, n_d, hpiece, width // QUARTERS), bf),
            ((2, n_a, n_a, piece, hid), bf),
            ((QUARTERS, n_a, n_a, hpiece, width // QUARTERS), bf),
            ((2, n_a, piece, hid), bf),
            ((QUARTERS, n_a, hpiece, width // QUARTERS), bf),
            ((2, n_a, piece, hid), bf),
            ((QUARTERS, n_a, hpiece, width // QUARTERS), bf),
        ]
        held = sum(math.prod(shape) * jnp.dtype(kind).itemsize for shape, kind in scratch)
        args = (tokens, out_grad, expert_ids.T, gate_probs.T, w_gate, w_up, w_down)
        made = pl.pallas_call(
            functools.partial(kernel, n_e, n_a, n_b),
            out_shape=(
                jax.ShapeDtypeStruct((1, piece, hid), bf),
                jax.ShapeDtypeStruct((1, piece, hid), bf),
                jax.ShapeDtypeStruct((1, hpiece, width), bf),
            ),
            in_specs=[hbm] * 7,
            out_specs=(vmem, vmem, vmem),
            scratch_shapes=[pltpu.VMEM(shape, kind) for shape, kind in scratch]
            + [
                dma((7,)),
                dma((2 + QUARTERS, 2, n_e)),
                dma((2 + QUARTERS, n_e)),
                dma((2 + QUARTERS, n_e)),
                dma((2 + QUARTERS, n_d)),
                dma((2 + QUARTERS, n_a, n_a)),
                dma((2 + QUARTERS, n_a)),
                dma((2 + QUARTERS, n_a)),
            ],
            compiler_params=pltpu.CompilerParams(
                collective_id=0, has_side_effects=True, vmem_limit_bytes=held + (10 << 20)
            ),
        )(*(pltpu.with_memory_space_constraint(x, pltpu.HBM) for x in args))
        return write_out(made)

    spread = P(("expert", "dp"), None)
    return jax.shard_map(
        step,
        mesh=mesh,
        in_specs=(spread, spread, spread, spread) + (P("expert", None, None),) * 3,
        out_specs=(P("expert", "dp", None),) * 3,
        check_vma=False,
    )
```
